512 devices in a mesh: seq: 32 (over y, z_hi, core), head: 16 (over x, z_lo).
Axes of the slice: x: 4, y: 8, z: 8 (z_hi: 2, z_lo: 4; z = z_hi * 4 + z_lo), core: 2. Of those that a mesh axis runs over, the one named last changes fastest.
Arguments:
- query_new: bfloat16 [4096, 6144], P('seq', 'head'), may hold values from -18 to 18
- key_new: bfloat16 [4096, 6144], P('seq', 'head'), may hold values from -4 to 4
- value_new: bfloat16 [4096, 6144], P('seq', 'head'), may hold values from -6 to 6
- cache_keys: bfloat16 [2048, 6144], P(('seq', 'head')), may hold values from -448 to 448
- cache_values: bfloat16 [2048, 6144], P(('seq', 'head')), may hold values from -448 to 448
- key_exponent: int32 [512, 48], P(('seq', 'head')), may hold values from -9 to -6
- value_exponent: int32 [512, 48], P(('seq', 'head')), may hold values from -9 to -6
- block_mask: int32 [64, 64], replicated, may hold values 0 or 1
Outputs:
- attended: bfloat16 [4096, 6144], P('seq', 'head')
The draws below stay inside these ranges and needn't reach their ends.
All inputs are finite; a program needn't handle non-finite values.
Results may differ from the reference program's by a relative error of at most 0.0065.
Values may be sent and summed in bfloat16 or wider, within the bound.
A program may use at most 64 MiB of HBM per device.

```python
import math
import jax
import jax.numpy as jnp
from jax import lax

H = 48
DH = 128
D = 6144
QBLK = 64
CBLK = 32
SBLK = 4
NEW = 4096
CACHE = 2048


def draw_query_new(key, part):
    own_key = jax.random.fold_in(key, 11)
    values = jax.random.truncated_normal(own_key, -6.0, 6.0, (NEW, D), jnp.float32)
    return values.astype(jnp.bfloat16)


def draw_key_new(key, part):
    own_key = jax.random.fold_in(key, 13)
    values = jax.random.truncated_normal(own_key, -4.0, 4.0, (NEW, D), jnp.float32)
    return values.astype(jnp.bfloat16)


def with_ends(drawn, key, low, largest):
    spot = [jax.random.randint(jax.random.fold_in(key, axis), (), 0, length) for axis, length in enumerate(drawn.shape)]
    widest = drawn.shape.index(max(drawn.shape))
    beside = spot[:widest] + [(spot[widest] + 1) % drawn.shape[widest]] + spot[widest + 1:]
    return drawn.at[tuple(spot)].set(low).at[tuple(beside)].set(largest)


def block_levels(key, extent, shards, low, top_value):
    loudness = 1.0
    for axis_at, shards_of in shards:
        steps = jax.random.uniform(jax.random.fold_in(jax.random.fold_in(key, 6), axis_at), (shards_of,), jnp.float32, low / len(shards), top_value / len(shards))
        loudness = loudness * jnp.repeat(jnp.exp(steps), extent[axis_at] // shards_of).reshape((-1,) + (1,) * (len(extent) - 1 - axis_at))
    return loudness


def scatter_about(rng, dims, spread, reach, shards=(), kind=jnp.bfloat16):
    values = jax.random.normal(rng, dims, jnp.float32) * spread
    if len(shards) > 0:
        values = block_levels(rng, dims, shards, -0.22, 0.18) * values
    return jnp.clip(values, min=-reach, max=reach).astype(kind)


def setup_inputs(seed: int = 0) -> dict:
    seeds = jax.random.split(jax.random.key(seed), 9)
    return {
        "query_new": draw_query_new(jax.random.fold_in(seeds[8], 71), 0),
        "key_new": draw_key_new(jax.random.fold_in(seeds[8], 71), 0),
        "value_new": scatter_about(seeds[2], (NEW, D), 1.0, 6.0, ((0, 32), (1, 16))),
        "cache_keys": scatter_about(seeds[3], (CACHE, D), 64.0, 448.0, ((0, 512),)),
        "cache_values": scatter_about(seeds[4], (CACHE, D), 64.0, 448.0, ((0, 512),)),
        "key_exponent": with_ends(jax.random.randint(seeds[5], (CACHE // SBLK, H), -9, -5), jax.random.fold_in(seeds[5], 1), -9, (-5) - 1).astype(jnp.int32),
        "value_exponent": with_ends(jax.random.randint(seeds[6], (CACHE // SBLK, H), -9, -5), jax.random.fold_in(seeds[6], 1), -9, (-5) - 1).astype(jnp.int32),
        "block_mask": with_ends((jax.random.randint(seeds[7], (NEW // QBLK, CACHE // CBLK), 0, 4) < 3).astype(jnp.int32), jax.random.fold_in(seeds[7], 1), 0, 1),
    }


def dequantize(mantissa, exponent):
    block_rows = mantissa.shape[0] // SBLK
    factor = jnp.exp2(exponent.astype(jnp.float32))
    scaled = mantissa.astype(jnp.float32).reshape(block_rows, SBLK, H, DH) * factor[:, None, :, None]
    return scaled.reshape(mantissa.shape).astype(jnp.bfloat16)

def reference(query_new, key_new, value_new, cache_keys, cache_values, key_exponent, value_exponent, block_mask):
    keys = jnp.concatenate([dequantize(cache_keys, key_exponent), key_new], axis=0)
    values = jnp.concatenate([dequantize(cache_values, value_exponent), value_new], axis=0)
    cache_allow = jnp.repeat(block_mask, CBLK, axis=1)
    allow_blocks = jnp.concatenate([cache_allow, jnp.ones((NEW // QBLK, NEW), jnp.int32)], axis=1) == 1
    key_count = keys.shape[0]
    rows_blk = min(512, NEW)
    block_count = NEW // rows_blk
    inv_root = 1.0 / math.sqrt(DH)

    def one_block(position):
        head_index = position // block_count
        block_index = position % block_count
        zero_start = jnp.int32(0)
        query_rows = lax.dynamic_slice(query_new, (block_index * rows_blk, head_index * DH), (rows_blk, DH))
        key_head = lax.dynamic_slice(keys, (zero_start, head_index * DH), (key_count, DH))
        value_head = lax.dynamic_slice(values, (zero_start, head_index * DH), (key_count, DH))
        scores = jnp.dot(query_rows, key_head.T, preferred_element_type=jnp.float32) * inv_root
        allowed = lax.dynamic_slice(allow_blocks, (block_index * (rows_blk // QBLK), zero_start), (rows_blk // QBLK, key_count))
        allowed = jnp.repeat(allowed, QBLK, axis=0)
        peak = lax.optimization_barrier(jnp.max(jnp.where(allowed, scores, -jnp.inf), axis=1, keepdims=True))
        raised = jnp.where(allowed, jnp.exp(scores - peak), 0.0)
        total = lax.optimization_barrier(jnp.sum(raised, axis=1, keepdims=True))
        weights = raised.astype(jnp.bfloat16)
        result = jnp.dot(weights, value_head, preferred_element_type=jnp.float32) / total
        return result.astype(jnp.bfloat16)
    results = lax.map(one_block, jnp.arange(H * block_count, dtype=jnp.int32))
    return results.reshape(H, NEW, DH).transpose(1, 0, 2).reshape(NEW, H * DH)
```

```python
import math

import jax
import jax.numpy as jnp
from jax import lax
from jax.experimental import pallas as pl
from jax.experimental.pallas import tpu as pltpu
from jax.sharding import PartitionSpec as P

DH = 128
QBLK = 64
CBLK = 32
SBLK = 4
HPD = 3
NY = 8
TOK = 128
CTOK = 64
MESH = pl.DeviceIdType.MESH
NEG = -1e30
SCALE = math.log2(math.e) / math.sqrt(DH)


def kernel(
    heads_n,
    seq_n,
    q_in,
    k_in,
    v_in,
    ck_in,
    cv_in,
    ke_in,
    ve_in,
    mask_in,
    o_ref,
    qb,
    kn,
    kc,
    dq,
    rc,
    stage,
    bias,
    acc,
    mx,
    sm,
    osend,
    orecv,
    ssend,
    srecv,
    loc_sem,
    a2a_s,
    a2a_r,
    q_s,
    q_r,
    n_s,
    n_r,
    nsib_s,
    nsib_r,
    c_s,
    c_r,
    csib_s,
    csib_r,
    o_s,
    o_r,
    st_s,
    st_r,
):
    seq = lax.axis_index("seq")
    head = lax.axis_index("head")
    y = seq // 4
    zh = (seq // 2) % 2
    core = seq % 2
    right = (lax.rem(seq + 4, seq_n), head)
    left = (lax.rem(seq + seq_n - 4, seq_n), head)
    zpart = (seq + 2 - 4 * zh, head)
    sib = (seq + 1 - 2 * core, head)

    local = []
    for h in range(HPD):
        cols = pl.ds(h * DH, DH)
        local.append(pltpu.make_async_copy(k_in.at[:, cols], kn.at[0, h, 0, 0:TOK], loc_sem.at[0, h]))
        local.append(pltpu.make_async_copy(v_in.at[:, cols], kn.at[0, h, 1, 0:TOK], loc_sem.at[1, h]))
    for h in range(HPD):
        cols = pl.ds(h * DH, DH)
        local.append(pltpu.make_async_copy(q_in.at[:, cols], qb.at[h, 0:TOK], loc_sem.at[2, h]))
    for cp in local:
        cp.start()

    barrier = pltpu.get_barrier_semaphore()
    for peer in (right, left, sib, zpart):
        pl.semaphore_signal(barrier, inc=1, device_id=peer, device_id_type=MESH)
    for r in range(1, heads_n):
        peer = (seq, lax.rem(head + r, heads_n))
        pl.semaphore_signal(barrier, inc=1, device_id=peer, device_id_type=MESH)

    for side, (c_in, e_in) in enumerate(((ck_in, ke_in), (cv_in, ve_in))):
        factor = jnp.exp2(e_in[...].astype(jnp.float32))
        for g in range(heads_n * HPD):
            cols = slice(g * DH, (g + 1) * DH)
            row = c_in[:, cols].astype(jnp.float32) * factor[:, g : g + 1]
            h = g % HPD
            dq[g // HPD, side, :, h * DH : (h + 1) * DH] = row.astype(jnp.bfloat16).astype(dq.dtype)

    mask = mask_in[...].astype(jnp.bfloat16)
    nq, nk = mask_in.shape
    qrow = lax.broadcasted_iota(jnp.int32, (2 * TOK, nq), 0)
    qcol = lax.broadcasted_iota(jnp.int32, (2 * TOK, nq), 1)
    zz = jnp.where(qrow < TOK, zh, 1 - zh)
    per = TOK // QBLK
    qblk = (y * 4 + zz * 2 + core) * per + (qrow & (TOK - 1)) // QBLK
    pick_q = jnp.where(qblk == qcol, 1.0, 0.0).astype(jnp.bfloat16)
    krow = lax.broadcasted_iota(jnp.int32, (nk, NY * 2 * CTOK), 0)
    kcol = lax.broadcasted_iota(jnp.int32, (nk, NY * 2 * CTOK), 1)
    rel = kcol // (2 * CTOK)
    other = (kcol // CTOK) & 1
    src_core = core + other * (1 - 2 * core)
    src = ((y + rel) & (NY - 1)) * 4 + zh * 2 + src_core
    kblk = src * (CTOK // CBLK) + (kcol & (CTOK - 1)) // CBLK
    pick_k = jnp.where(kblk == krow, 1.0, 0.0).astype(jnp.bfloat16)
    rows_mask = jnp.dot(pick_q, mask, preferred_element_type=jnp.float32).astype(jnp.bfloat16)
    seen = jnp.dot(rows_mask, pick_k, preferred_element_type=jnp.float32)
    bias[...] = jnp.where(seen > 0.5, 0.0, NEG)

    for cp in local:
        cp.wait()
    pl.semaphore_wait(barrier, 4 + heads_n - 1)

    def remote(src_ref, dst_ref, send, recv, peer):
        return pltpu.make_async_remote_copy(
            src_ref=src_ref, dst_ref=dst_ref, send_sem=send, recv_sem=recv, device_id=peer, device_id_type=MESH
        )

    def n_copy(src_rel, dst_rel, h, half, peer):
        if half is None:
            a, b, k = kn.at[src_rel, h, :, 0:TOK], kn.at[dst_rel, h, :, 0:TOK], 0
        else:
            a, b, k = kn.at[src_rel, h, half, 0:TOK], kn.at[dst_rel, h, half, 0:TOK], half
        return remote(a, b, n_s.at[dst_rel, h, k], n_r.at[dst_rel, h, k], peer)

    def n_sib(rel_y, h):
        return remote(
            kn.at[rel_y, h, :, 0:TOK], kn.at[rel_y, h, :, TOK : 2 * TOK], nsib_s.at[rel_y, h], nsib_r.at[rel_y, h], sib
        )

    def c_copy(src_rel, dst_rel, half, peer):
        if half is None:
            a, b, k = kc.at[src_rel, :, :, 0:CTOK], kc.at[dst_rel, :, :, 0:CTOK], 0
        else:
            a, b, k = kc.at[src_rel, :, half, 0:CTOK], kc.at[dst_rel, :, half, 0:CTOK], half
        return remote(a, b, c_s.at[dst_rel, k], c_r.at[dst_rel, k], peer)

    def c_sib(rel_y):
        return remote(
            kc.at[rel_y, :, :, 0:CTOK], kc.at[rel_y, :, :, CTOK : 2 * CTOK], csib_s.at[rel_y], csib_r.at[rel_y], sib
        )

    def q_copy(h):
        return remote(qb.at[h, 0:TOK], qb.at[h, TOK : 2 * TOK], q_s.at[h], q_r.at[h], zpart)

    def a2a_copy(r):
        dst = lax.rem(head + r, heads_n)
        return remote(dq.at[dst], rc.at[head], a2a_s.at[r], a2a_r.at[r], (seq, dst))

    def o_copy(h):
        return remote(osend.at[h], orecv.at[h], o_s.at[h], o_r.at[h], zpart)

    def st_copy(h):
        return remote(ssend.at[h], srecv.at[h], st_s.at[h], st_r.at[h], zpart)

    n_copy(0, 7, 0, None, right).start()
    n_copy(0, 1, 0, None, left).start()
    for r in range(1, heads_n):
        a2a_copy(r).start()
    for h in range(1, HPD):
        n_copy(0, 7, h, None, right).start()
        n_copy(0, 1, h, None, left).start()
    for h in range(HPD):
        q_copy(h).start()
    for h in range(HPD):
        n_sib(0, h).start()
    own = pltpu.make_async_copy(dq.at[head], rc.at[head], a2a_s.at[0])
    own.start()

    def attend(h, parts, first=False):
        q = qb[h]
        scores = []
        for keys, add in parts:
            s = lax.dot_general(q, keys[0], (((1,), (1,)), ((), ())), preferred_element_type=jnp.float32)
            if add is not None:
                s = s + add
            scores.append(s)
        top = None
        for s in scores:
            t = jnp.max(s, axis=1, keepdims=True)
            top = t if top is None else jnp.maximum(top, t)
        if not first:
            before = mx[h][:, 0:1]
            top = jnp.maximum(top, before)
        shift = top * SCALE
        total = None
        out = None
        for s, (keys, add) in zip(scores, parts):
            p = jnp.exp2(s * SCALE - shift)
            t = jnp.sum(p, axis=1, keepdims=True)
            o = jnp.dot(p.astype(jnp.bfloat16), keys[1], preferred_element_type=jnp.float32)
            total = t if total is None else total + t
            out = o if out is None else out + o
        if not first:
            back = jnp.exp2(before * SCALE - shift)
            total = sm[h][:, 0:1] * back + total
            out = acc[h] * back + out
        mx[h] = jnp.broadcast_to(top, (2 * TOK, DH))
        sm[h] = jnp.broadcast_to(total, (2 * TOK, DH))
        acc[h] = out

    def n_part(rel_y, h):
        return ((kn[rel_y, h, 0], kn[rel_y, h, 1]), None)

    def c_part(rel_y, h):
        return ((kc[rel_y, h, 0], kc[rel_y, h, 1]), bias[:, rel_y * 2 * CTOK : (rel_y + 1) * 2 * CTOK])

    def each_head(body):
        def step(h, carry):
            body(h)
            return carry

        lax.fori_loop(0, HPD, step, 0)

    def pass_n1(h):
        n_copy(0, 7, h, None, right).wait_recv()
        n_copy(7, 6, h, None, right).start()
        n_sib(7, h).start()
        n_copy(0, 1, h, None, left).wait_recv()
        n_copy(1, 2, h, None, left).start()
        n_sib(1, h).start()

    each_head(pass_n1)

    own.wait()
    for r in range(1, heads_n):
        a2a_copy(r).wait_recv()
    for side in range(2):
        for s in range(heads_n):
            stage[side, s * SBLK : (s + 1) * SBLK, :] = rc[s, side].astype(jnp.float32)
        for h in range(HPD):
            kc[0, h, side, 0:CTOK] = stage[side, :, h * DH : (h + 1) * DH].astype(jnp.bfloat16)

    def work0(h):
        n_sib(0, h).wait_recv()
        q_copy(h).wait_recv()
        attend(h, [n_part(0, h)], first=True)

    each_head(work0)

    c_copy(0, 7, None, right).start()
    c_copy(0, 1, None, left).start()
    c_sib(0).start()

    def work1(h):
        n_copy(7, 6, h, None, right).wait_recv()
        n_copy(6, 5, h, None, right).start()
        n_sib(6, h).start()
        n_copy(1, 2, h, None, left).wait_recv()
        n_copy(2, 3, h, None, left).start()
        n_sib(2, h).start()
        n_sib(7, h).wait_recv()
        n_sib(1, h).wait_recv()
        attend(h, [n_part(7, h), n_part(1, h)])

    each_head(work1)

    c_copy(0, 7, None, right).wait_recv()
    c_copy(7, 6, None, right).start()
    c_sib(7).start()
    c_copy(0, 1, None, left).wait_recv()
    c_copy(1, 2, None, left).start()
    c_sib(1).start()

    def work2(h):
        n_copy(6, 5, h, None, right).wait_recv()
        n_copy(5, 4, h, 0, right).start()
        n_sib(5, h).start()
        n_copy(2, 3, h, None, left).wait_recv()
        n_copy(3, 4, h, 1, left).start()
        n_sib(3, h).start()
        n_sib(6, h).wait_recv()
        n_sib(2, h).wait_recv()
        attend(h, [n_part(6, h), n_part(2, h)])

    each_head(work2)

    c_copy(7, 6, None, right).wait_recv()
    c_copy(6, 5, None, right).start()
    c_sib(6).start()
    c_copy(1, 2, None, left).wait_recv()
    c_copy(2, 3, None, left).start()
    c_sib(2).start()
    c_sib(0).wait_recv()
    c_sib(7).wait_recv()
    c_sib(1).wait_recv()

    def work3(h):
        n_copy(5, 4, h, 0, right).wait_recv()
        n_copy(3, 4, h, 1, left).wait_recv()
        n_sib(4, h).start()
        n_sib(5, h).wait_recv()
        n_sib(3, h).wait_recv()
        attend(h, [n_part(5, h), n_part(3, h), c_part(0, h)])

    each_head(work3)

    c_copy(6, 5, None, right).wait_recv()
    c_copy(5, 4, 0, right).start()
    c_sib(5).start()
    c_copy(2, 3, None, left).wait_recv()
    c_copy(3, 4, 1, left).start()
    c_sib(3).start()
    c_sib(6).wait_recv()
    c_sib(2).wait_recv()

    def work4(h):
        n_sib(4, h).wait_recv()
        attend(h, [n_part(4, h), c_part(7, h), c_part(1, h), c_part(6, h), c_part(2, h)])

    each_head(work4)

    c_copy(5, 4, 0, right).wait_recv()
    c_copy(3, 4, 1, left).wait_recv()
    c_sib(4).start()
    c_sib(5).wait_recv()
    c_sib(3).wait_recv()
    c_sib(4).wait_recv()

    def work5(h):
        attend(h, [c_part(5, h), c_part(3, h), c_part(4, h)])
        total = sm[h, TOK : 2 * TOK]
        osend[h] = (acc[h, TOK : 2 * TOK] / total).astype(osend.dtype)
        ssend[h, 0] = mx[h, TOK : 2 * TOK].T[0:8]
        ssend[h, 1] = total.T[0:8]
        o_copy(h).start()
        st_copy(h).start()

    each_head(work5)

    for h in range(HPD):
        o_copy(h).wait_recv()
        st_copy(h).wait_recv()
        m0 = mx[h, 0:TOK]
        l0 = sm[h, 0:TOK]
        m1 = jnp.concatenate([srecv[h, 0]] * (DH // 8), axis=0).T
        l1 = jnp.concatenate([srecv[h, 1]] * (DH // 8), axis=0).T
        m = jnp.maximum(m0, m1)
        w0 = jnp.exp2((m0 - m) * SCALE)
        w1 = jnp.exp2((m1 - m) * SCALE) * l1
        full = acc[h, 0:TOK] * w0 + orecv[h].astype(jnp.float32) * w1
        o_ref[:, h * DH : (h + 1) * DH] = (full / (l0 * w0 + w1)).astype(o_ref.dtype)

    for r in range(1, heads_n):
        a2a_copy(r).wait_send()

    def drain(h):
        n_copy(0, 7, h, None, right).wait_send()
        n_copy(7, 6, h, None, right).wait_send()
        n_copy(6, 5, h, None, right).wait_send()
        n_copy(5, 4, h, 0, right).wait_send()
        n_copy(0, 1, h, None, left).wait_send()
        n_copy(1, 2, h, None, left).wait_send()
        n_copy(2, 3, h, None, left).wait_send()
        n_copy(3, 4, h, 1, left).wait_send()
        for rel_y in range(NY):
            n_sib(rel_y, h).wait_send()
        q_copy(h).wait_send()
        o_copy(h).wait_send()
        st_copy(h).wait_send()

    each_head(drain)
    c_copy(0, 7, None, right).wait_send()
    c_copy(7, 6, None, right).wait_send()
    c_copy(6, 5, None, right).wait_send()
    c_copy(5, 4, 0, right).wait_send()
    c_copy(0, 1, None, left).wait_send()
    c_copy(1, 2, None, left).wait_send()
    c_copy(2, 3, None, left).wait_send()
    c_copy(3, 4, 1, left).wait_send()
    for rel_y in range(NY):
        c_sib(rel_y).wait_send()


def per_device(heads_n, seq_n, *args):
    import functools

    anywhere = pl.BlockSpec(memory_space=pl.ANY)
    vmem = pl.BlockSpec(memory_space=pltpu.VMEM)
    dma = pltpu.SemaphoreType.DMA
    f32, bf16 = jnp.float32, jnp.bfloat16
    return pl.pallas_call(
        functools.partial(kernel, heads_n, seq_n),
        out_shape=jax.ShapeDtypeStruct((TOK, HPD * DH), bf16),
        in_specs=[anywhere] * 3 + [vmem] * 5,
        out_specs=vmem,
        scratch_shapes=[
            pltpu.VMEM((HPD, 2 * TOK, DH), bf16),
            pltpu.VMEM((NY, HPD, 2, 2 * TOK, DH), bf16),
            pltpu.VMEM((NY, HPD, 2, 2 * CTOK, DH), bf16),
            pltpu.VMEM((heads_n, 2, SBLK, HPD * DH), bf16),
            pltpu.VMEM((heads_n, 2, SBLK, HPD * DH), bf16),
            pltpu.VMEM((2, CTOK, HPD * DH), f32),
            pltpu.VMEM((2 * TOK, NY * 2 * CTOK), f32),
            pltpu.VMEM((HPD, 2 * TOK, DH), f32),
            pltpu.VMEM((HPD, 2 * TOK, DH), f32),
            pltpu.VMEM((HPD, 2 * TOK, DH), f32),
            pltpu.VMEM((HPD, TOK, DH), bf16),
            pltpu.VMEM((HPD, TOK, DH), bf16),
            pltpu.VMEM((HPD, 2, 8, DH), f32),
            pltpu.VMEM((HPD, 2, 8, DH), f32),
            dma((3, HPD)),
            dma((heads_n,)),
            dma((heads_n,)),
            dma((HPD,)),
            dma((HPD,)),
            dma((NY, HPD, 2)),
            dma((NY, HPD, 2)),
            dma((NY, HPD)),
            dma((NY, HPD)),
            dma((NY, 2)),
            dma((NY, 2)),
            dma((NY,)),
            dma((NY,)),
            dma((HPD,)),
            dma((HPD,)),
            dma((HPD,)),
            dma((HPD,)),
        ],
        compiler_params=pltpu.CompilerParams(
            collective_id=0, has_side_effects=True, vmem_limit_bytes=60 * 1024 * 1024
        ),
        name="attend_ring",
    )(*args)


def solution(mesh):
    import functools

    both = P(("seq", "head"), None)
    own = P("seq", "head")
    return jax.shard_map(
        functools.partial(per_device, mesh.shape["head"], mesh.shape["seq"]),
        mesh=mesh,
        in_specs=(own, own, own, both, both, both, both, P()),
        out_specs=own,
        check_vma=False,
    )
```

```python
import math

import jax
import jax.numpy as jnp
from jax import lax
from jax.experimental import pallas as pl
from jax.experimental.pallas import tpu as pltpu
from jax.sharding import PartitionSpec as P

DH = 128
QBLK = 64
CBLK = 32
SBLK = 4
HPD = 3
NY = 8
TOK = 128
CTOK = 64
MESH = pl.DeviceIdType.MESH
NEG = -1e30
SCALE = math.log2(math.e) / math.sqrt(DH)


def kernel(
    heads_n,
    seq_n,
    q_in,
    k_in,
    v_in,
    ck_in,
    cv_in,
    ke_in,
    ve_in,
    mask_in,
    o_ref,
    qb,
    kn,
    kc,
    dq,
    rc,
    stage,
    bias,
    acc,
    mx,
    sm,
    osend,
    orecv,
    ssend,
    srecv,
    ck,
    cv,
    ke,
    ve,
    mask_v,
    loc_sem,
    in_sem,
    in_kernel,
    a2a_s,
    a2a_r,
    q_s,
    q_r,
    n_s,
    n_r,
    nsib_s,
    nsib_r,
    c_s,
    c_r,
    csib_s,
    csib_r,
    o_s,
    o_r,
    st_s,
    st_r,
):
    seq = lax.axis_index("seq")
    head = lax.axis_index("head")
    y = seq // 4
    zh = (seq // 2) % 2
    core = seq % 2
    right = (lax.rem(seq + 4, seq_n), head)
    left = (lax.rem(seq + seq_n - 4, seq_n), head)
    zpart = (seq + 2 - 4 * zh, head)
    sib = (seq + 1 - 2 * core, head)

    local = []
    for h in range(HPD):
        cols = pl.ds(h * DH, DH)
        local.append(pltpu.make_async_copy(k_in.at[:, cols], kn.at[0, h, 0, 0:TOK], loc_sem.at[0, h]))
        local.append(pltpu.make_async_copy(v_in.at[:, cols], kn.at[0, h, 1, 0:TOK], loc_sem.at[1, h]))
    for h in range(HPD):
        cols = pl.ds(h * DH, DH)
        local.append(pltpu.make_async_copy(q_in.at[:, cols], qb.at[h, 0:TOK], loc_sem.at[2, h]))
    small = [
        pltpu.make_async_copy(a, b, in_sem.at[i])
        for i, (a, b) in enumerate(((ck_in, ck), (cv_in, cv), (ke_in, ke), (ve_in, ve), (mask_in, mask_v)))
    ]
    for cp in local + small:
        cp.start()

    barrier = pltpu.get_barrier_semaphore()
    for peer in (right, left, sib):
        pl.semaphore_signal(barrier, inc=1, device_id=peer, device_id_type=MESH)
    for r in range(1, heads_n):
        peer = (seq, lax.rem(head + r, heads_n))
        pl.semaphore_signal(barrier, inc=1, device_id=peer, device_id_type=MESH)


    @pl.when(zh == 0)
    def _():
        pl.semaphore_signal(barrier, inc=1, device_id=zpart, device_id_type=MESH)

    pl.semaphore_wait(barrier, 3 + heads_n - 1 + zh)

    def remote(src_ref, dst_ref, send, recv, peer):
        return pltpu.make_async_remote_copy(
            src_ref=src_ref, dst_ref=dst_ref, send_sem=send, recv_sem=recv, device_id=peer, device_id_type=MESH
        )

    def n_copy(src_rel, dst_rel, h, half, peer):
        if half is None:
            a, b, k = kn.at[src_rel, h, :, 0:TOK], kn.at[dst_rel, h, :, 0:TOK], 0
        else:
            a, b, k = kn.at[src_rel, h, half, 0:TOK], kn.at[dst_rel, h, half, 0:TOK], half
        return remote(a, b, n_s.at[dst_rel, h, k], n_r.at[dst_rel, h, k], peer)

    def n_sib(rel_y, h):
        return remote(
            kn.at[rel_y, h, :, 0:TOK], kn.at[rel_y, h, :, TOK : 2 * TOK], nsib_s.at[rel_y, h], nsib_r.at[rel_y, h], sib
        )

    def c_copy(src_rel, dst_rel, h, half, peer):
        if half is None:
            a, b, k = kc.at[src_rel, h, :, 0:CTOK], kc.at[dst_rel, h, :, 0:CTOK], 0
        else:
            a, b, k = kc.at[src_rel, h, half, 0:CTOK], kc.at[dst_rel, h, half, 0:CTOK], half
        return remote(a, b, c_s.at[dst_rel, h, k], c_r.at[dst_rel, h, k], peer)

    def c_sib(rel_y, h):
        return remote(
            kc.at[rel_y, h, :, 0:CTOK], kc.at[rel_y, h, :, CTOK : 2 * CTOK], csib_s.at[rel_y, h], csib_r.at[rel_y, h], sib
        )

    def q_copy(h):
        return remote(qb.at[h, 0:TOK], qb.at[h, TOK : 2 * TOK], q_s.at[h], q_r.at[h], zpart)

    def a2a_copy(r):
        dst = lax.rem(head + r, heads_n)
        return remote(dq.at[dst], rc.at[head], a2a_s.at[r], a2a_r.at[r], (seq, dst))

    def o_copy(h):
        return remote(osend.at[h], orecv.at[h], o_s.at[h], o_r.at[h], zpart)

    def st_copy(h):
        return remote(ssend.at[h], srecv.at[h], st_s.at[h], st_r.at[h], zpart)

    for h in range(HPD):
        for cp in (local[2 * h], local[2 * h + 1]):
            cp.wait()
        n_copy(0, 7, h, None, right).start()
        n_copy(0, 1, h, None, left).start()
    for h in range(HPD):
        local[2 * HPD + h].wait()

    @pl.when(zh == 1)
    def _():
        pl.semaphore_signal(in_kernel, inc=1, device_id=zpart, device_id_type=MESH)
        for h in range(HPD):
            q_copy(h).start()

    for cp in small[:4]:
        cp.wait()
    for side, (c_in, e_in) in enumerate(((ck, ke), (cv, ve))):
        factor = jnp.exp2(e_in[...].astype(jnp.float32))
        for g in range(heads_n * HPD):
            cols = slice(g * DH, (g + 1) * DH)
            row = c_in[:, cols].astype(jnp.float32) * factor[:, g : g + 1]
            h = g % HPD
            dq[g // HPD, side, :, h * DH : (h + 1) * DH] = row.astype(jnp.bfloat16).astype(dq.dtype)

    for r in range(1, heads_n):
        a2a_copy(r).start()
    own = pltpu.make_async_copy(dq.at[head], rc.at[head], a2a_s.at[0])
    own.start()
    for h in range(HPD):
        n_sib(0, h).start()
    small[4].wait()
    mask = mask_v[...].astype(jnp.bfloat16)
    nq, nk = mask_v.shape
    qrow = lax.broadcasted_iota(jnp.int32, (2 * TOK, nq), 0)
    qcol = lax.broadcasted_iota(jnp.int32, (2 * TOK, nq), 1)
    zz = jnp.where(qrow < TOK, zh, 1 - zh)
    per = TOK // QBLK
    qblk = (y * 4 + zz * 2 + core) * per + (qrow & (TOK - 1)) // QBLK
    pick_q = jnp.where(qblk == qcol, 1.0, 0.0).astype(jnp.bfloat16)
    krow = lax.broadcasted_iota(jnp.int32, (nk, NY * 2 * CTOK), 0)
    kcol = lax.broadcasted_iota(jnp.int32, (nk, NY * 2 * CTOK), 1)
    rel = kcol // (2 * CTOK)
    other = (kcol // CTOK) & 1
    src_core = core + other * (1 - 2 * core)
    src = ((y + rel) & (NY - 1)) * 4 + zh * 2 + src_core
    kblk = src * (CTOK // CBLK) + (kcol & (CTOK - 1)) // CBLK
    pick_k = jnp.where(kblk == krow, 1.0, 0.0).astype(jnp.bfloat16)
    rows_mask = jnp.dot(pick_q, mask, preferred_element_type=jnp.float32).astype(jnp.bfloat16)
    seen = jnp.dot(rows_mask, pick_k, preferred_element_type=jnp.float32)
    bias[...] = jnp.where(seen > 0.5, 0.0, NEG)

    def attend(h, parts, rows=slice(0, 2 * TOK), first=False):
        q = qb[h, rows]
        scores = []
        for keys, add in parts:
            s = lax.dot_general(q, keys[0], (((1,), (1,)), ((), ())), preferred_element_type=jnp.float32)
            if add is not None:
                s = s + add[rows]
            scores.append(s)
        top = None
        for s in scores:
            t = jnp.max(s, axis=1, keepdims=True)
            top = t if top is None else jnp.maximum(top, t)
        if not first:
            before = mx[h, rows][:, 0:1]
            top = jnp.maximum(top, before)
        shift = top * SCALE
        total = None
        out = None
        for s, (keys, add) in zip(scores, parts):
            p = jnp.exp2(s * SCALE - shift)
            t = jnp.sum(p, axis=1, keepdims=True)
            o = jnp.dot(p.astype(jnp.bfloat16), keys[1], preferred_element_type=jnp.float32)
            total = t if total is None else total + t
            out = o if out is None else out + o
        if not first:
            back = jnp.exp2(before * SCALE - shift)
            total = sm[h, rows][:, 0:1] * back + total
            out = acc[h, rows] * back + out
        mx[h, rows] = jnp.broadcast_to(top, out.shape)
        sm[h, rows] = jnp.broadcast_to(total, out.shape)
        acc[h, rows] = out

    def n_part(rel_y, h):
        return ((kn[rel_y, h, 0], kn[rel_y, h, 1]), None)

    def c_part(rel_y, h):
        return ((kc[rel_y, h, 0], kc[rel_y, h, 1]), bias.at[:, rel_y * 2 * CTOK : (rel_y + 1) * 2 * CTOK])

    def relay(copy, to_sib, d, h):
        back_r = 8 - d + 1 if d > 1 else 0
        copy(back_r, 8 - d, h, None, right).wait_recv()
        if d < 3:
            copy(8 - d, 7 - d, h, None, right).start()
        else:
            copy(5, 4, h, 0, right).start()
        to_sib(8 - d, h).start()
        copy(d - 1, d, h, None, left).wait_recv()
        if d < 3:
            copy(d, d + 1, h, None, left).start()
        else:
            copy(3, 4, h, 1, left).start()
        to_sib(d, h).start()

    def last(h):
        for copy, to_sib in ((n_copy, n_sib), (c_copy, c_sib)):
            copy(5, 4, h, 0, right).wait_recv()
            copy(3, 4, h, 1, left).wait_recv()
            to_sib(4, h).start()

    def need(h, new=(), cached=()):
        for rel_y in new:
            n_sib(rel_y, h).wait_recv()
        for rel_y in cached:
            c_sib(rel_y, h).wait_recv()

    for h in range(HPD):
        relay(n_copy, n_sib, 1, h)

    own.wait()
    for r in range(1, heads_n):
        a2a_copy(r).wait_recv()
    for side in range(2):
        for s in range(heads_n):
            stage[side, s * SBLK : (s + 1) * SBLK, :] = rc[s, side].astype(jnp.float32)
    for h in range(HPD):
        for side in range(2):
            kc[0, h, side, 0:CTOK] = stage[side, :, h * DH : (h + 1) * DH].astype(jnp.bfloat16)
    relay(n_copy, n_sib, 2, 0)
    for h in range(HPD):
        c_copy(0, 7, h, None, right).start()
        c_copy(0, 1, h, None, left).start()
        c_sib(0, h).start()

    mine, theirs = slice(0, TOK), slice(TOK, 2 * TOK)

    def work_a(h, rows):
        attend(h, [n_part(0, h), n_part(7, h), n_part(1, h)], rows=rows, first=True)

    def work_b(h):
        need(h, new=(6, 2), cached=(0, 7, 1))
        attend(h, [n_part(6, h), n_part(2, h), c_part(0, h), c_part(7, h), c_part(1, h)])

    def work_d(h):
        need(h, new=(5, 3), cached=(6, 2))
        attend(h, [n_part(5, h), n_part(3, h), c_part(6, h), c_part(2, h)])

    def work_f(h):
        need(h, cached=(5, 3))
        attend(h, [c_part(5, h), c_part(3, h)])

    def work_g(h):
        need(h, new=(4,), cached=(4,))
        attend(h, [n_part(4, h), c_part(4, h)], rows=theirs)
        total = sm[h, theirs]
        osend[h] = (acc[h, theirs] / total).astype(osend.dtype)
        ssend[h, 0:1] = mx[h, theirs].T[0:1]
        ssend[h, 1:2] = total.T[0:1]
        o_copy(h).start()
        st_copy(h).start()

    @pl.when(zh == 0)
    def _():
        pl.semaphore_wait(in_kernel, 1)
        for h in range(HPD):
            q_copy(h).start()

    for h in range(HPD):
        need(h, new=(0, 7, 1))
        work_a(h, mine)
    for h in range(HPD):
        relay(c_copy, c_sib, 1, h)
    relay(n_copy, n_sib, 2, 1)
    relay(n_copy, n_sib, 2, 2)
    for h in range(HPD):
        q_copy(h).wait_recv()
        work_a(h, theirs)
    for h in range(HPD):
        relay(c_copy, c_sib, 2, h)
    relay(n_copy, n_sib, 3, 0)
    work_b(0)
    work_d(0)
    work_b(1)
    relay(c_copy, c_sib, 3, 0)
    relay(n_copy, n_sib, 3, 1)
    relay(c_copy, c_sib, 3, 1)
    relay(n_copy, n_sib, 3, 2)
    relay(c_copy, c_sib, 3, 2)
    work_b(2)
    work_d(1)
    work_f(0)
    last(0)
    work_d(2)
    work_f(1)
    last(1)
    work_f(2)
    work_g(0)
    last(2)
    work_g(1)
    work_g(2)
    for h in range(HPD):
        attend(h, [n_part(4, h), c_part(4, h)], rows=mine)

    for h in range(HPD):
        o_copy(h).wait_recv()
        st_copy(h).wait_recv()
        m0 = mx[h, 0:TOK]
        l0 = sm[h, 0:TOK]
        m1 = jnp.broadcast_to(srecv[h, 0:1], (TOK, DH)).T
        l1 = jnp.broadcast_to(srecv[h, 1:2], (TOK, DH)).T
        m = jnp.maximum(m0, m1)
        w0 = jnp.exp2((m0 - m) * SCALE)
        w1 = jnp.exp2((m1 - m) * SCALE) * l1
        full = acc[h, 0:TOK] * w0 + orecv[h].astype(jnp.float32) * w1
        o_ref[:, h * DH : (h + 1) * DH] = (full / (l0 * w0 + w1)).astype(o_ref.dtype)

    for r in range(1, heads_n):
        a2a_copy(r).wait_send()
    for h in range(HPD):
        for copy, to_sib in ((n_copy, n_sib), (c_copy, c_sib)):
            for d in range(3):
                copy(8 - d if d else 0, 7 - d, h, None, right).wait_send()
                copy(d, d + 1, h, None, left).wait_send()
            copy(5, 4, h, 0, right).wait_send()
            copy(3, 4, h, 1, left).wait_send()
            for rel_y in range(NY):
                to_sib(rel_y, h).wait_send()
        q_copy(h).wait_send()
        o_copy(h).wait_send()
        st_copy(h).wait_send()


def per_device(heads_n, seq_n, *args):
    import functools

    hbm = pl.BlockSpec(memory_space=pltpu.HBM)
    vmem = pl.BlockSpec(memory_space=pltpu.VMEM)
    dma = pltpu.SemaphoreType.DMA
    f32, bf16 = jnp.float32, jnp.bfloat16
    return pl.pallas_call(
        functools.partial(kernel, heads_n, seq_n),
        out_shape=jax.ShapeDtypeStruct((TOK, HPD * DH), bf16),
        in_specs=[hbm] * 8,
        out_specs=vmem,
        scratch_shapes=[
            pltpu.VMEM((HPD, 2 * TOK, DH), bf16),
            pltpu.VMEM((NY, HPD, 2, 2 * TOK, DH), bf16),
            pltpu.VMEM((NY, HPD, 2, 2 * CTOK, DH), bf16),
            pltpu.VMEM((heads_n, 2, SBLK, HPD * DH), bf16),
            pltpu.VMEM((heads_n, 2, SBLK, HPD * DH), bf16),
            pltpu.VMEM((2, CTOK, HPD * DH), f32),
            pltpu.VMEM((2 * TOK, NY * 2 * CTOK), f32),
            pltpu.VMEM((HPD, 2 * TOK, DH), f32),
            pltpu.VMEM((HPD, 2 * TOK, DH), f32),
            pltpu.VMEM((HPD, 2 * TOK, DH), f32),
            pltpu.VMEM((HPD, TOK, DH), bf16),
            pltpu.VMEM((HPD, TOK, DH), bf16),
            pltpu.VMEM((HPD, 2, DH), f32),
            pltpu.VMEM((HPD, 2, DH), f32),
            pltpu.VMEM((SBLK, heads_n * HPD * DH), bf16),
            pltpu.VMEM((SBLK, heads_n * HPD * DH), bf16),
            pltpu.VMEM((1, heads_n * HPD), jnp.int32),
            pltpu.VMEM((1, heads_n * HPD), jnp.int32),
            pltpu.VMEM(args[7].shape, jnp.int32),
            dma((3, HPD)),
            dma((5,)),
            pltpu.SemaphoreType.REGULAR,
            dma((heads_n,)),
            dma((heads_n,)),
            dma((HPD,)),
            dma((HPD,)),
            dma((NY, HPD, 2)),
            dma((NY, HPD, 2)),
            dma((NY, HPD)),
            dma((NY, HPD)),
            dma((NY, HPD, 2)),
            dma((NY, HPD, 2)),
            dma((NY, HPD)),
            dma((NY, HPD)),
            dma((HPD,)),
            dma((HPD,)),
            dma((HPD,)),
            dma((HPD,)),
        ],
        compiler_params=pltpu.CompilerParams(
            collective_id=0, has_side_effects=True, vmem_limit_bytes=60 * 1024 * 1024
        ),
        name="attend_ring",
    )(*args)


def solution(mesh):
    import functools

    both = P(("seq", "head"), None)
    own = P("seq", "head")
    return jax.shard_map(
        functools.partial(per_device, mesh.shape["head"], mesh.shape["seq"]),
        mesh=mesh,
        in_specs=(own, own, own, both, both, both, both, P()),
        out_specs=own,
        check_vma=False,
    )
```

```python
import math

import jax
import jax.numpy as jnp
from jax import lax
from jax.experimental import pallas as pl
from jax.experimental.pallas import tpu as pltpu
from jax.sharding import PartitionSpec as P

DH = 128
QBLK = 64
CBLK = 32
SBLK = 4
HPD = 3
NY = 8
ZLO = 4
TOK = 128
CTOK = 64
MESH = pl.DeviceIdType.MESH
NEG = -1e30
SCALE = math.log2(math.e) / math.sqrt(DH)


def kernel(
    heads_n,
    seq_n,
    q_in,
    k_in,
    v_in,
    ck_in,
    cv_in,
    ke_in,
    ve_in,
    mask_in,
    o_ref,
    qb,
    kn,
    dq,
    rc,
    stage,
    bias,
    acc,
    mx,
    sm,
    osend,
    orecv,
    ssend,
    srecv,
    ck,
    cv,
    ke,
    ve,
    mask_v,
    loc_sem,
    in_sem,
    in_kernel,
    in_peers,
    a2a_s,
    a2a_r,
    q_s,
    q_r,
    n_s,
    n_r,
    nsib_s,
    nsib_r,
    o_s,
    o_r,
    st_s,
    st_r,
):
    seq = lax.axis_index("seq")
    head = lax.axis_index("head")
    y = seq // 4
    zh = (seq // 2) % 2
    core = seq % 2
    right = (lax.rem(seq + 4, seq_n), head)
    left = (lax.rem(seq + seq_n - 4, seq_n), head)
    zpart = (seq + 2 - 4 * zh, head)
    sib = (seq + 1 - 2 * core, head)

    local = []
    for h in range(HPD):
        cols = pl.ds(h * DH, DH)
        local.append(pltpu.make_async_copy(k_in.at[:, cols], kn.at[0, h, 0, 0:TOK], loc_sem.at[0, h]))
        local.append(pltpu.make_async_copy(v_in.at[:, cols], kn.at[0, h, 1, 0:TOK], loc_sem.at[1, h]))
    for h in range(HPD):
        cols = pl.ds(h * DH, DH)
        local.append(pltpu.make_async_copy(q_in.at[:, cols], qb.at[h, 0:TOK], loc_sem.at[2, h]))
    small = [
        pltpu.make_async_copy(a, b, in_sem.at[i])
        for i, (a, b) in enumerate(((ck_in, ck), (cv_in, cv), (ke_in, ke), (ve_in, ve), (mask_in, mask_v)))
    ]
    for cp in local + small:
        cp.start()

    first_half, second_half = zh == 0, zh == 1
    zl = lax.rem(head, ZLO)
    peers = [lax.rem(head + r, heads_n) for r in range(heads_n)]
    barrier = pltpu.get_barrier_semaphore()
    for peer in (right, left, sib):
        pl.semaphore_signal(barrier, inc=1, device_id=peer, device_id_type=MESH)

    @pl.when(first_half)
    def _():
        for p in peers[1:]:

            @pl.when(lax.rem(p, ZLO) >= zl)
            def _():
                pl.semaphore_signal(barrier, inc=1, device_id=(seq, p), device_id_type=MESH)

        for p in peers:
            pl.semaphore_signal(barrier, inc=1, device_id=(zpart[0], p), device_id_type=MESH)

    def dequantize():
        for cp in small[:4]:
            cp.wait()
        for side, (c_in, e_in) in enumerate(((ck, ke), (cv, ve))):
            factor = jnp.exp2(e_in[...].astype(jnp.float32))
            for g in range(heads_n * HPD):
                cols = slice(g * DH, (g + 1) * DH)
                row = c_in[:, cols].astype(jnp.float32) * factor[:, g : g + 1]
                h = g % HPD
                dq[g // HPD, side, :, h * DH : (h + 1) * DH] = row.astype(jnp.bfloat16).astype(dq.dtype)

    @pl.when(second_half)
    def _():
        dequantize()

    level = heads_n // ZLO
    pl.semaphore_wait(barrier, 3 + (1 - zh) * (level * (zl + 1) - 1) + zh * heads_n)

    def remote(src_ref, dst_ref, send, recv, peer):
        return pltpu.make_async_remote_copy(
            src_ref=src_ref, dst_ref=dst_ref, send_sem=send, recv_sem=recv, device_id=peer, device_id_type=MESH
        )

    def n_copy(src_rel, dst_rel, h, half, peer):
        if half is None:
            a, b, k = kn.at[src_rel, h, :, 0:TOK], kn.at[dst_rel, h, :, 0:TOK], 0
        else:
            a, b, k = kn.at[src_rel, h, half, 0:TOK], kn.at[dst_rel, h, half, 0:TOK], half
        return remote(a, b, n_s.at[dst_rel, h, k], n_r.at[dst_rel, h, k], peer)

    def n_sib(rel_y, h):
        return remote(
            kn.at[rel_y, h, :, 0:TOK], kn.at[rel_y, h, :, TOK : 2 * TOK], nsib_s.at[rel_y, h], nsib_r.at[rel_y, h], sib
        )

    def q_copy(h):
        return remote(qb.at[h, 0:TOK], qb.at[h, TOK : 2 * TOK], q_s.at[h], q_r.at[h], zpart)

    def a2a_near(r):
        return remote(dq.at[peers[r]], rc.at[0, head], a2a_s.at[r], a2a_r.at[0, r], (seq, peers[r]))

    def a2a_far(r):
        return remote(dq.at[peers[r]], rc.at[1, head], a2a_s.at[r], a2a_r.at[1, r], (zpart[0], peers[r]))

    def o_copy(h):
        return remote(osend.at[h], orecv.at[h], o_s.at[h], o_r.at[h], zpart)

    def st_copy(h):
        return remote(ssend.at[h], srecv.at[h], st_s.at[h], st_r.at[h], zpart)

    @pl.when(second_half)
    def _():
        for r in range(heads_n):
            a2a_far(r).start()

    for h in range(HPD):
        for cp in (local[2 * h], local[2 * h + 1]):
            cp.wait()
        n_copy(0, 7, h, None, right).start()
        n_copy(0, 1, h, None, left).start()
    for h in range(HPD):
        n_sib(0, h).start()
    for h in range(HPD):
        local[2 * HPD + h].wait()

    @pl.when(second_half)
    def _():
        pl.semaphore_signal(in_kernel, inc=1, device_id=zpart, device_id_type=MESH)
        for h in range(HPD):
            q_copy(h).start()

    @pl.when(first_half)
    def _():
        for p in peers[1:]:

            @pl.when(lax.rem(p, ZLO) < zl)
            def _():
                pl.semaphore_signal(in_peers, inc=1, device_id=(seq, p), device_id_type=MESH)

    small[4].wait()

    @pl.when(first_half)
    def _():
        dequantize()

    def attend(h, parts, rows=slice(0, 2 * TOK), first=False):
        q = qb[h, rows]
        scores = []
        for keys, add in parts:
            s = lax.dot_general(q, keys[0], (((1,), (1,)), ((), ())), preferred_element_type=jnp.float32)
            if add is not None:
                s = s + add[rows]
            scores.append(s)
        top = None
        for s in scores:
            t = jnp.max(s, axis=1, keepdims=True)
            top = t if top is None else jnp.maximum(top, t)
        if not first:
            before = mx[h, rows][:, 0:1]
            top = jnp.maximum(top, before)
        shift = top * SCALE
        total = None
        out = None
        for s, (keys, add) in zip(scores, parts):
            p = jnp.exp2(s * SCALE - shift)
            t = jnp.sum(p, axis=1, keepdims=True)
            o = jnp.dot(p.astype(jnp.bfloat16), keys[1], preferred_element_type=jnp.float32)
            total = t if total is None else total + t
            out = o if out is None else out + o
        if not first:
            back = jnp.exp2(before * SCALE - shift)
            total = sm[h, rows][:, 0:1] * back + total
            out = acc[h, rows] * back + out
        mx[h, rows] = jnp.broadcast_to(top, out.shape)
        sm[h, rows] = jnp.broadcast_to(total, out.shape)
        acc[h, rows] = out

    def n_part(rel_y, h):
        return ((kn[rel_y, h, 0], kn[rel_y, h, 1]), None)

    def c_part(rel_y, h):
        return (
            (kn[rel_y, HPD + h, 0], kn[rel_y, HPD + h, 1]),
            bias.at[:, rel_y * 4 * CTOK : (rel_y + 1) * 4 * CTOK],
        )

    def relay(d, h):
        back_r = 8 - d + 1 if d > 1 else 0
        n_copy(back_r, 8 - d, h, None, right).wait_recv()
        if d < 3:
            n_copy(8 - d, 7 - d, h, None, right).start()
        else:
            n_copy(5, 4, h, 0, right).start()
        n_sib(8 - d, h).start()
        n_copy(d - 1, d, h, None, left).wait_recv()
        if d < 3:
            n_copy(d, d + 1, h, None, left).start()
        else:
            n_copy(3, 4, h, 1, left).start()
        n_sib(d, h).start()

    def last(h):
        n_copy(5, 4, h, 0, right).wait_recv()
        n_copy(3, 4, h, 1, left).wait_recv()
        n_sib(4, h).start()

    def need(h, rels):
        for rel_y in rels:
            n_sib(rel_y, h).wait_recv()

    every, mine, theirs = slice(0, 2 * TOK), slice(0, TOK), slice(TOK, 2 * TOK)

    def new_work(h, rels, rows=every, first=False):
        attend(h, [n_part(rel_y, h) for rel_y in rels], rows=rows, first=first)

    def cached_work(h, rels, rows=every):
        attend(h, [c_part(rel_y, h) for rel_y in rels], rows=rows)

    def share(h):
        total = sm[h, theirs]
        osend[h] = (acc[h, theirs] / total).astype(osend.dtype)
        ssend[h, 0:1] = mx[h, theirs].T[0:1]
        ssend[h, 1:2] = total.T[0:1]
        o_copy(h).start()
        st_copy(h).start()

    for h in range(HPD):
        relay(1, h)

    @pl.when(first_half)
    def _():

        @pl.when(zl < ZLO - 1)
        def _():
            pl.semaphore_wait(in_peers, level * (ZLO - 1 - zl))

        for r in range(1, heads_n):
            a2a_near(r).start()
        pltpu.make_async_copy(dq.at[head], rc.at[0, head], a2a_s.at[0]).start()

    relay(2, 0)

    @pl.when(first_half)
    def _():
        mask = mask_v[...].astype(jnp.bfloat16)
        nq, nk = mask_v.shape
        qrow = lax.broadcasted_iota(jnp.int32, (2 * TOK, nq), 0)
        qcol = lax.broadcasted_iota(jnp.int32, (2 * TOK, nq), 1)
        zz = jnp.where(qrow < TOK, zh, 1 - zh)
        per = TOK // QBLK
        qblk = (y * 4 + zz * 2 + core) * per + (qrow & (TOK - 1)) // QBLK
        pick_q = jnp.where(qblk == qcol, 1.0, 0.0).astype(jnp.bfloat16)
        krow = lax.broadcasted_iota(jnp.int32, (nk, NY * 4 * CTOK), 0)
        kcol = lax.broadcasted_iota(jnp.int32, (nk, NY * 4 * CTOK), 1)
        rel = kcol // (4 * CTOK)
        other = (kcol // (2 * CTOK)) & 1
        src_core = core + other * (1 - 2 * core)
        src = ((y + rel) & (NY - 1)) * 4 + ((kcol // CTOK) & 1) * 2 + src_core
        kblk = src * (CTOK // CBLK) + (kcol & (CTOK - 1)) // CBLK
        pick_k = jnp.where(kblk == krow, 1.0, 0.0).astype(jnp.bfloat16)
        rows_mask = jnp.dot(pick_q, mask, preferred_element_type=jnp.float32).astype(jnp.bfloat16)
        seen = jnp.dot(rows_mask, pick_k, preferred_element_type=jnp.float32)
        bias[...] = jnp.where(seen > 0.5, 0.0, NEG)

    relay(2, 1)
    relay(2, 2)

    for h in range(HPD):
        need(h, (0, 7, 1))
        new_work(h, (0, 7, 1), rows=mine, first=True)
    for h in range(HPD):
        relay(3, h)

    @pl.when(first_half)
    def _():
        pltpu.make_async_copy(dq.at[head], rc.at[0, head], a2a_s.at[0]).wait()
        for r in range(1, heads_n):
            a2a_near(r).wait_recv()
        for r in range(heads_n):
            a2a_far(r).wait_recv()
        for side in range(2):
            for half in range(2):
                for src in range(heads_n):
                    row = half * CTOK + src * SBLK
                    stage[side, row : row + SBLK, :] = rc[half, src, side].astype(jnp.float32)
        for h in range(HPD):
            for side in range(2):
                kn[0, HPD + h, side, 0:TOK] = stage[side, :, h * DH : (h + 1) * DH].astype(jnp.bfloat16)
        for h in range(HPD, 2 * HPD):
            n_copy(0, 7, h, None, right).start()
            n_copy(0, 1, h, None, left).start()
            n_sib(0, h).start()

    @pl.when(first_half)
    def _():
        pl.semaphore_wait(in_kernel, 1)
        for h in range(HPD):
            q_copy(h).start()

    for h in range(HPD):
        last(h)
    for h in range(HPD):
        q_copy(h).wait_recv()
        new_work(h, (0, 7, 1), rows=theirs, first=True)

    @pl.when(second_half)
    def _():
        for h in range(HPD):
            need(h, (6, 2, 5, 3))
            new_work(h, (6, 2, 5, 3))
            need(h, (4,))
            new_work(h, (4,))
            share(h)

    @pl.when(first_half)
    def _():
        for h in range(HPD):
            relay(1, HPD + h)
            need(h, (6, 2, 5, 3))
            new_work(h, (6, 2, 5, 3))
        relay(2, HPD)
        for h in range(HPD):
            need(h, (4,))
            new_work(h, (4,))
        relay(2, HPD + 1)
        need(HPD, (0, 7, 1))
        cached_work(0, (0, 7, 1))
        relay(2, HPD + 2)
        need(HPD + 1, (0, 7, 1))
        cached_work(1, (0, 7, 1))
        relay(3, HPD)
        need(HPD + 2, (0, 7, 1))
        cached_work(2, (0, 7, 1))
        relay(3, HPD + 1)
        need(HPD, (6, 2))
        cached_work(0, (6, 2))
        relay(3, HPD + 2)
        for h in range(1, HPD):
            need(HPD + h, (6, 2))
            cached_work(h, (6, 2))
        last(HPD)
        need(HPD, (5, 3))
        cached_work(0, (5, 3))
        last(HPD + 1)
        need(HPD + 1, (5, 3))
        cached_work(1, (5, 3))
        last(HPD + 2)
        need(HPD + 2, (5, 3))
        cached_work(2, (5, 3))
        for h in range(HPD):
            need(HPD + h, (4,))
            cached_work(h, (4,), rows=theirs)
            share(h)
        for h in range(HPD):
            cached_work(h, (4,), rows=mine)

    for h in range(HPD):
        o_copy(h).wait_recv()
        st_copy(h).wait_recv()
        m0 = mx[h, 0:TOK]
        l0 = sm[h, 0:TOK]
        m1 = jnp.broadcast_to(srecv[h, 0:1], (TOK, DH)).T
        l1 = jnp.broadcast_to(srecv[h, 1:2], (TOK, DH)).T
        m = jnp.maximum(m0, m1)
        w0 = jnp.exp2((m0 - m) * SCALE)
        w1 = jnp.exp2((m1 - m) * SCALE) * l1
        full = acc[h, 0:TOK] * w0 + orecv[h].astype(jnp.float32) * w1
        o_ref[:, h * DH : (h + 1) * DH] = (full / (l0 * w0 + w1)).astype(o_ref.dtype)

    def drain(h):
        for d in range(3):
            n_copy(8 - d if d else 0, 7 - d, h, None, right).wait_send()
            n_copy(d, d + 1, h, None, left).wait_send()
        n_copy(5, 4, h, 0, right).wait_send()
        n_copy(3, 4, h, 1, left).wait_send()
        for rel_y in range(NY):
            n_sib(rel_y, h).wait_send()

    for h in range(HPD):
        drain(h)
        q_copy(h).wait_send()
        o_copy(h).wait_send()
        st_copy(h).wait_send()

    @pl.when(first_half)
    def _():
        for r in range(1, heads_n):
            a2a_near(r).wait_send()
        for h in range(HPD, 2 * HPD):
            drain(h)

    @pl.when(second_half)
    def _():
        for r in range(heads_n):
            a2a_far(r).wait_send()


def per_device(heads_n, seq_n, *args):
    import functools

    hbm = pl.BlockSpec(memory_space=pltpu.HBM)
    vmem = pl.BlockSpec(memory_space=pltpu.VMEM)
    dma = pltpu.SemaphoreType.DMA
    f32, bf16 = jnp.float32, jnp.bfloat16
    return pl.pallas_call(
        functools.partial(kernel, heads_n, seq_n),
        out_shape=jax.ShapeDtypeStruct((TOK, HPD * DH), bf16),
        in_specs=[hbm] * 8,
        out_specs=vmem,
        scratch_shapes=[
            pltpu.VMEM((HPD, 2 * TOK, DH), bf16),
            pltpu.VMEM((NY, 2 * HPD, 2, 2 * TOK, DH), bf16),
            pltpu.VMEM((heads_n, 2, SBLK, HPD * DH), bf16),
            pltpu.VMEM((2, heads_n, 2, SBLK, HPD * DH), bf16),
            pltpu.VMEM((2, 2 * CTOK, HPD * DH), f32),
            pltpu.VMEM((2 * TOK, NY * 4 * CTOK), f32),
            pltpu.VMEM((HPD, 2 * TOK, DH), f32),
            pltpu.VMEM((HPD, 2 * TOK, DH), f32),
            pltpu.VMEM((HPD, 2 * TOK, DH), f32),
            pltpu.VMEM((HPD, TOK, DH), bf16),
            pltpu.VMEM((HPD, TOK, DH), bf16),
            pltpu.VMEM((HPD, 2, DH), f32),
            pltpu.VMEM((HPD, 2, DH), f32),
            pltpu.VMEM((SBLK, heads_n * HPD * DH), bf16),
            pltpu.VMEM((SBLK, heads_n * HPD * DH), bf16),
            pltpu.VMEM((1, heads_n * HPD), jnp.int32),
            pltpu.VMEM((1, heads_n * HPD), jnp.int32),
            pltpu.VMEM(args[7].shape, jnp.int32),
            dma((3, HPD)),
            dma((5,)),
            pltpu.SemaphoreType.REGULAR,
            pltpu.SemaphoreType.REGULAR,
            dma((heads_n,)),
            dma((2, heads_n)),
            dma((HPD,)),
            dma((HPD,)),
            dma((NY, 2 * HPD, 2)),
            dma((NY, 2 * HPD, 2)),
            dma((NY, 2 * HPD)),
            dma((NY, 2 * HPD)),
            dma((HPD,)),
            dma((HPD,)),
            dma((HPD,)),
            dma((HPD,)),
        ],
        compiler_params=pltpu.CompilerParams(
            collective_id=0, has_side_effects=True, vmem_limit_bytes=60 * 1024 * 1024
        ),
        name="attend_ring",
    )(*args)


def solution(mesh):
    import functools

    both = P(("seq", "head"), None)
    own = P("seq", "head")
    return jax.shard_map(
        functools.partial(per_device, mesh.shape["head"], mesh.shape["seq"]),
        mesh=mesh,
        in_specs=(own, own, own, both, both, both, both, P()),
        out_specs=own,
        check_vma=False,
    )
```

```python
import math

import jax
import jax.numpy as jnp
from jax import lax
from jax.experimental import pallas as pl
from jax.experimental.pallas import tpu as pltpu
from jax.sharding import PartitionSpec as P

DH = 128
QBLK = 64
CBLK = 32
SBLK = 4
HPD = 3
NY = 8
ZLO = 4
TOK = 128
CTOK = 64
MESH = pl.DeviceIdType.MESH
NEG = -1e30
SCALE = math.log2(math.e) / math.sqrt(DH)


def kernel(
    heads_n,
    seq_n,
    q_in,
    k_in,
    v_in,
    ck_in,
    cv_in,
    ke_in,
    ve_in,
    mask_in,
    o_ref,
    qb,
    kn,
    dq,
    rc,
    stage,
    bias,
    acc,
    mx,
    sm,
    osend,
    orecv,
    ssend,
    srecv,
    ck,
    cv,
    ke,
    ve,
    mask_v,
    loc_sem,
    in_sem,
    in_kernel,
    in_peers,
    a2a_s,
    a2a_r,
    q_s,
    q_r,
    n_s,
    n_r,
    nsib_s,
    nsib_r,
    o_s,
    o_r,
    st_s,
    st_r,
):
    seq = lax.axis_index("seq")
    head = lax.axis_index("head")
    y = seq // 4
    zh = (seq // 2) % 2
    core = seq % 2
    right = (lax.rem(seq + 4, seq_n), head)
    left = (lax.rem(seq + seq_n - 4, seq_n), head)
    zpart = (seq + 2 - 4 * zh, head)
    sib = (seq + 1 - 2 * core, head)

    local = []
    for h in range(HPD):
        cols = pl.ds(h * DH, DH)
        local.append(pltpu.make_async_copy(k_in.at[:, cols], kn.at[0, h, 0, 0:TOK], loc_sem.at[0, h]))
        local.append(pltpu.make_async_copy(v_in.at[:, cols], kn.at[0, h, 1, 0:TOK], loc_sem.at[1, h]))
    for h in range(HPD):
        cols = pl.ds(h * DH, DH)
        local.append(pltpu.make_async_copy(q_in.at[:, cols], qb.at[h, 0:TOK], loc_sem.at[2, h]))
    small = [
        pltpu.make_async_copy(a, b, in_sem.at[i])
        for i, (a, b) in enumerate(((ck_in, ck), (cv_in, cv), (ke_in, ke), (ve_in, ve), (mask_in, mask_v)))
    ]
    for cp in local + small:
        cp.start()

    first_half, second_half = zh == 0, zh == 1
    zl = lax.rem(head, ZLO)
    peers = [lax.rem(head + r, heads_n) for r in range(heads_n)]
    barrier = pltpu.get_barrier_semaphore()
    for peer in (right, left, sib):
        pl.semaphore_signal(barrier, inc=1, device_id=peer, device_id_type=MESH)

    @pl.when(first_half)
    def _():
        for p in peers[1:]:

            @pl.when(lax.rem(p, ZLO) >= zl)
            def _():
                pl.semaphore_signal(barrier, inc=1, device_id=(seq, p), device_id_type=MESH)

        for p in peers:
            pl.semaphore_signal(barrier, inc=1, device_id=(zpart[0], p), device_id_type=MESH)

    def dequantize():
        for cp in small[:4]:
            cp.wait()
        for side, (c_in, e_in) in enumerate(((ck, ke), (cv, ve))):
            factor = jnp.exp2(e_in[...].astype(jnp.float32))
            for g in range(heads_n * HPD):
                cols = slice(g * DH, (g + 1) * DH)
                row = c_in[:, cols].astype(jnp.float32) * factor[:, g : g + 1]
                h = g % HPD
                dq[g // HPD, side, :, h * DH : (h + 1) * DH] = row.astype(jnp.bfloat16).astype(dq.dtype)

    @pl.when(second_half)
    def _():
        dequantize()

    level = heads_n // ZLO
    pl.semaphore_wait(barrier, 3 + (1 - zh) * (level * (zl + 1) - 1) + zh * heads_n)

    def remote(src_ref, dst_ref, send, recv, peer):
        return pltpu.make_async_remote_copy(
            src_ref=src_ref, dst_ref=dst_ref, send_sem=send, recv_sem=recv, device_id=peer, device_id_type=MESH
        )

    def n_copy(src_rel, dst_rel, h, half, peer):
        if half is None:
            a, b, k = kn.at[src_rel, h, :, 0:TOK], kn.at[dst_rel, h, :, 0:TOK], 0
        else:
            a, b, k = kn.at[src_rel, h, half, 0:TOK], kn.at[dst_rel, h, half, 0:TOK], half
        return remote(a, b, n_s.at[dst_rel, h, k], n_r.at[dst_rel, h, k], peer)

    def n_sib(rel_y, h):
        return remote(
            kn.at[rel_y, h, :, 0:TOK], kn.at[rel_y, h, :, TOK : 2 * TOK], nsib_s.at[rel_y, h], nsib_r.at[rel_y, h], sib
        )

    def q_copy(h):
        return remote(qb.at[h, 0:TOK], qb.at[h, TOK : 2 * TOK], q_s.at[h], q_r.at[h], zpart)

    def a2a_near(r):
        return remote(dq.at[peers[r]], rc.at[0, head], a2a_s.at[r], a2a_r.at[0, r], (seq, peers[r]))

    def a2a_far(r):
        return remote(dq.at[peers[r]], rc.at[1, head], a2a_s.at[r], a2a_r.at[1, r], (zpart[0], peers[r]))

    def o_copy(h):
        return remote(osend.at[h], orecv.at[h], o_s.at[h], o_r.at[h], zpart)

    def st_copy(h):
        return remote(ssend.at[h], srecv.at[h], st_s.at[h], st_r.at[h], zpart)

    @pl.when(second_half)
    def _():
        for r in range(heads_n):
            a2a_far(r).start()

    for h in range(HPD):
        for cp in (local[2 * h], local[2 * h + 1]):
            cp.wait()
        n_copy(0, 7, h, None, right).start()
        n_copy(0, 1, h, None, left).start()
    for h in range(HPD):
        n_sib(0, h).start()
    for h in range(HPD):
        local[2 * HPD + h].wait()

    @pl.when(second_half)
    def _():
        pl.semaphore_signal(in_kernel, inc=1, device_id=zpart, device_id_type=MESH)
        for h in range(HPD):
            q_copy(h).start()

    @pl.when(first_half)
    def _():
        for p in peers[1:]:

            @pl.when(lax.rem(p, ZLO) < zl)
            def _():
                pl.semaphore_signal(in_peers, inc=1, device_id=(seq, p), device_id_type=MESH)

    small[4].wait()

    @pl.when(first_half)
    def _():
        dequantize()

    def attend(h, parts, rows=slice(0, 2 * TOK), first=False):
        q = qb[h, rows]
        scores = []
        for keys, add in parts:
            s = lax.dot_general(q, keys[0], (((1,), (1,)), ((), ())), preferred_element_type=jnp.float32)
            if add is not None:
                s = s + add[rows]
            scores.append(s)
        top = None
        for s in scores:
            t = jnp.max(s, axis=1, keepdims=True)
            top = t if top is None else jnp.maximum(top, t)
        if not first:
            before = mx[h, rows][:, 0:1]
            top = jnp.maximum(top, before)
        shift = top * SCALE
        total = None
        out = None
        for s, (keys, add) in zip(scores, parts):
            p = jnp.exp2(s * SCALE - shift)
            t = jnp.sum(p, axis=1, keepdims=True)
            o = jnp.dot(p.astype(jnp.bfloat16), keys[1], preferred_element_type=jnp.float32)
            total = t if total is None else total + t
            out = o if out is None else out + o
        if not first:
            back = jnp.exp2(before * SCALE - shift)
            total = sm[h, rows][:, 0:1] * back + total
            out = acc[h, rows] * back + out
        mx[h, rows] = jnp.broadcast_to(top, out.shape)
        sm[h, rows] = jnp.broadcast_to(total, out.shape)
        acc[h, rows] = out

    def n_part(rel_y, h):
        return ((kn[rel_y, h, 0], kn[rel_y, h, 1]), None)

    def c_part(rel_y, h):
        return (
            (kn[rel_y, HPD + h, 0], kn[rel_y, HPD + h, 1]),
            bias.at[:, rel_y * 4 * CTOK : (rel_y + 1) * 4 * CTOK],
        )

    def relay(d, h):
        back_r = 8 - d + 1 if d > 1 else 0
        n_copy(back_r, 8 - d, h, None, right).wait_recv()
        if d < 3:
            n_copy(8 - d, 7 - d, h, None, right).start()
        else:
            n_copy(5, 4, h, 0, right).start()
        n_sib(8 - d, h).start()
        n_copy(d - 1, d, h, None, left).wait_recv()
        if d < 3:
            n_copy(d, d + 1, h, None, left).start()
        else:
            n_copy(3, 4, h, 1, left).start()
        n_sib(d, h).start()

    def last(h):
        n_copy(5, 4, h, 0, right).wait_recv()
        n_copy(3, 4, h, 1, left).wait_recv()
        n_sib(4, h).start()

    def need(h, rels):
        for rel_y in rels:
            n_sib(rel_y, h).wait_recv()

    every, mine, theirs = slice(0, 2 * TOK), slice(0, TOK), slice(TOK, 2 * TOK)

    def new_work(h, rels, rows=every, first=False):
        attend(h, [n_part(rel_y, h) for rel_y in rels], rows=rows, first=first)

    def cached_work(h, rels, rows=every):
        attend(h, [c_part(rel_y, h) for rel_y in rels], rows=rows)

    def share(h):
        total = sm[h, theirs]
        osend[h] = (acc[h, theirs] / total).astype(osend.dtype)
        ssend[h, 0:1] = mx[h, theirs].T[0:1]
        ssend[h, 1:2] = total.T[0:1]
        o_copy(h).start()
        st_copy(h).start()

    for h in range(HPD):
        relay(1, h)

    @pl.when(first_half)
    def _():

        @pl.when(zl < ZLO - 1)
        def _():
            pl.semaphore_wait(in_peers, level * (ZLO - 1 - zl))

        for r in range(1, heads_n):
            a2a_near(r).start()
        pltpu.make_async_copy(dq.at[head], rc.at[0, head], a2a_s.at[0]).start()

    relay(2, 0)

    @pl.when(first_half)
    def _():
        mask = mask_v[...].astype(jnp.bfloat16)
        nq, nk = mask_v.shape
        qrow = lax.broadcasted_iota(jnp.int32, (2 * TOK, nq), 0)
        qcol = lax.broadcasted_iota(jnp.int32, (2 * TOK, nq), 1)
        zz = jnp.where(qrow < TOK, zh, 1 - zh)
        per = TOK // QBLK
        qblk = (y * 4 + zz * 2 + core) * per + (qrow & (TOK - 1)) // QBLK
        pick_q = jnp.where(qblk == qcol, 1.0, 0.0).astype(jnp.bfloat16)
        krow = lax.broadcasted_iota(jnp.int32, (nk, NY * 4 * CTOK), 0)
        kcol = lax.broadcasted_iota(jnp.int32, (nk, NY * 4 * CTOK), 1)
        rel = kcol // (4 * CTOK)
        other = (kcol // (2 * CTOK)) & 1
        src_core = core + other * (1 - 2 * core)
        src = ((y + rel) & (NY - 1)) * 4 + ((kcol // CTOK) & 1) * 2 + src_core
        kblk = src * (CTOK // CBLK) + (kcol & (CTOK - 1)) // CBLK
        pick_k = jnp.where(kblk == krow, 1.0, 0.0).astype(jnp.bfloat16)
        rows_mask = jnp.dot(pick_q, mask, preferred_element_type=jnp.float32).astype(jnp.bfloat16)
        seen = jnp.dot(rows_mask, pick_k, preferred_element_type=jnp.float32)
        bias[...] = jnp.where(seen > 0.5, 0.0, NEG)

    relay(2, 1)
    relay(2, 2)

    for h in range(HPD):
        need(h, (0, 7, 1))
        new_work(h, (0, 7, 1), rows=mine, first=True)
    for h in range(HPD):
        relay(3, h)
        need(h, (6, 2))
        new_work(h, (6, 2), rows=mine)

    @pl.when(first_half)
    def _():
        pltpu.make_async_copy(dq.at[head], rc.at[0, head], a2a_s.at[0]).wait()
        for r in range(1, heads_n):
            a2a_near(r).wait_recv()
        for r in range(heads_n):
            a2a_far(r).wait_recv()
        for side in range(2):
            for half in range(2):
                for src in range(heads_n):
                    row = half * CTOK + src * SBLK
                    stage[side, row : row + SBLK, :] = rc[half, src, side].astype(jnp.float32)
        for h in range(HPD):
            for side in range(2):
                kn[0, HPD + h, side, 0:TOK] = stage[side, :, h * DH : (h + 1) * DH].astype(jnp.bfloat16)
        for h in range(HPD, 2 * HPD):
            n_copy(0, 7, h, None, right).start()
            n_copy(0, 1, h, None, left).start()
            n_sib(0, h).start()

    @pl.when(first_half)
    def _():
        pl.semaphore_wait(in_kernel, 1)
        for h in range(HPD):
            q_copy(h).start()

    for h in range(HPD):
        last(h)
    for h in range(HPD):
        q_copy(h).wait_recv()
        new_work(h, (0, 7, 1), rows=theirs, first=True)

    @pl.when(second_half)
    def _():
        for h in range(HPD):
            need(h, (5, 3, 4))
            new_work(h, (6, 2, 5, 3, 4), rows=theirs)
            share(h)
        for h in range(HPD):
            new_work(h, (5, 3, 4), rows=mine)

    @pl.when(first_half)
    def _():
        for h in range(HPD):
            relay(1, HPD + h)
            need(h, (5, 3, 4))
            new_work(h, (6, 2, 5, 3, 4), rows=theirs)
        relay(2, HPD)
        for h in range(HPD):
            new_work(h, (5, 3, 4), rows=mine)
        relay(2, HPD + 1)
        need(HPD, (0, 7, 1))
        cached_work(0, (0, 7, 1))
        relay(2, HPD + 2)
        need(HPD + 1, (0, 7, 1))
        cached_work(1, (0, 7, 1))
        need(HPD, (6, 2))
        cached_work(0, (6, 2))
        relay(3, HPD)
        need(HPD + 2, (0, 7, 1))
        cached_work(2, (0, 7, 1))
        relay(3, HPD + 1)
        for h in range(1, HPD):
            need(HPD + h, (6, 2))
            cached_work(h, (6, 2))
        relay(3, HPD + 2)
        need(HPD, (5, 3))
        cached_work(0, (5, 3))
        last(HPD)
        need(HPD + 1, (5, 3))
        cached_work(1, (5, 3))
        last(HPD + 1)
        need(HPD, (4,))
        cached_work(0, (4,))
        share(0)
        last(HPD + 2)
        need(HPD + 2, (5, 3))
        cached_work(2, (5, 3))
        for h in range(1, HPD):
            need(HPD + h, (4,))
            cached_work(h, (4,))
            share(h)

    for h in range(HPD):
        o_copy(h).wait_recv()
        st_copy(h).wait_recv()
        m0 = mx[h, 0:TOK]
        l0 = sm[h, 0:TOK]
        m1 = jnp.broadcast_to(srecv[h, 0:1], (TOK, DH)).T
        l1 = jnp.broadcast_to(srecv[h, 1:2], (TOK, DH)).T
        m = jnp.maximum(m0, m1)
        w0 = jnp.exp2((m0 - m) * SCALE)
        w1 = jnp.exp2((m1 - m) * SCALE) * l1
        full = acc[h, 0:TOK] * w0 + orecv[h].astype(jnp.float32) * w1
        o_ref[:, h * DH : (h + 1) * DH] = (full / (l0 * w0 + w1)).astype(o_ref.dtype)

    def drain(h):
        for d in range(3):
            n_copy(8 - d if d else 0, 7 - d, h, None, right).wait_send()
            n_copy(d, d + 1, h, None, left).wait_send()
        n_copy(5, 4, h, 0, right).wait_send()
        n_copy(3, 4, h, 1, left).wait_send()
        for rel_y in range(NY):
            n_sib(rel_y, h).wait_send()

    for h in range(HPD):
        drain(h)
        q_copy(h).wait_send()
        o_copy(h).wait_send()
        st_copy(h).wait_send()

    @pl.when(first_half)
    def _():
        for r in range(1, heads_n):
            a2a_near(r).wait_send()
        for h in range(HPD, 2 * HPD):
            drain(h)

    @pl.when(second_half)
    def _():
        for r in range(heads_n):
            a2a_far(r).wait_send()


def per_device(heads_n, seq_n, *args):
    import functools

    hbm = pl.BlockSpec(memory_space=pltpu.HBM)
    vmem = pl.BlockSpec(memory_space=pltpu.VMEM)
    dma = pltpu.SemaphoreType.DMA
    f32, bf16 = jnp.float32, jnp.bfloat16
    return pl.pallas_call(
        functools.partial(kernel, heads_n, seq_n),
        out_shape=jax.ShapeDtypeStruct((TOK, HPD * DH), bf16),
        in_specs=[hbm] * 8,
        out_specs=vmem,
        scratch_shapes=[
            pltpu.VMEM((HPD, 2 * TOK, DH), bf16),
            pltpu.VMEM((NY, 2 * HPD, 2, 2 * TOK, DH), bf16),
            pltpu.VMEM((heads_n, 2, SBLK, HPD * DH), bf16),
            pltpu.VMEM((2, heads_n, 2, SBLK, HPD * DH), bf16),
            pltpu.VMEM((2, 2 * CTOK, HPD * DH), f32),
            pltpu.VMEM((2 * TOK, NY * 4 * CTOK), f32),
            pltpu.VMEM((HPD, 2 * TOK, DH), f32),
            pltpu.VMEM((HPD, 2 * TOK, DH), f32),
            pltpu.VMEM((HPD, 2 * TOK, DH), f32),
            pltpu.VMEM((HPD, TOK, DH), bf16),
            pltpu.VMEM((HPD, TOK, DH), bf16),
            pltpu.VMEM((HPD, 2, DH), f32),
            pltpu.VMEM((HPD, 2, DH), f32),
            pltpu.VMEM((SBLK, heads_n * HPD * DH), bf16),
            pltpu.VMEM((SBLK, heads_n * HPD * DH), bf16),
            pltpu.VMEM((1, heads_n * HPD), jnp.int32),
            pltpu.VMEM((1, heads_n * HPD), jnp.int32),
            pltpu.VMEM(args[7].shape, jnp.int32),
            dma((3, HPD)),
            dma((5,)),
            pltpu.SemaphoreType.REGULAR,
            pltpu.SemaphoreType.REGULAR,
            dma((heads_n,)),
            dma((2, heads_n)),
            dma((HPD,)),
            dma((HPD,)),
            dma((NY, 2 * HPD, 2)),
            dma((NY, 2 * HPD, 2)),
            dma((NY, 2 * HPD)),
            dma((NY, 2 * HPD)),
            dma((HPD,)),
            dma((HPD,)),
            dma((HPD,)),
            dma((HPD,)),
        ],
        compiler_params=pltpu.CompilerParams(
            collective_id=0, has_side_effects=True, vmem_limit_bytes=60 * 1024 * 1024
        ),
        name="attend_ring",
    )(*args)


def solution(mesh):
    import functools

    both = P(("seq", "head"), None)
    own = P("seq", "head")
    return jax.shard_map(
        functools.partial(per_device, mesh.shape["head"], mesh.shape["seq"]),
        mesh=mesh,
        in_specs=(own, own, own, both, both, both, both, P()),
        out_specs=own,
        check_vma=False,
    )
```
